32 devices in a mesh: group: 2 (over x), owner: 16 (over z, y, core).
Axes of the slice: x: 2, y: 2, z: 4, core: 2. Of those that a mesh axis runs over, the one named last changes fastest.
Arguments:
- tokens: bfloat16 [4096, 2048], P(('group', 'owner')), parts along dimension 0, may hold values from -6 to 6
- cotangent: bfloat16 [4096, 2048], P(('group', 'owner')), parts along dimension 0, may hold values from -6 to 6
- route_ids: int32 [4096, 3], P('group'), parts along dimension 0, may hold values from 0 to 15, as said below
- gate_probs: float32 [4096, 3], P(('group', 'owner')), parts along dimension 0, may hold values from 0.05 to 1
- w_gate: bfloat16 [16, 2048, 384], P('owner'), may hold values from -0.125 to 0.125
- w_up: bfloat16 [16, 2048, 384], P('owner'), may hold values from -0.125 to 0.125
- w_down: bfloat16 [16, 384, 2048], P('owner'), may hold values from -0.3125 to 0.3125
Outputs:
- expert_out: bfloat16 [4096, 2048], P(('group', 'owner')), parts along dimension 0
- grad_tokens: bfloat16 [4096, 2048], P(('group', 'owner')), parts along dimension 0
- grad_gates: float32 [4096, 3], P(('group', 'owner')), parts along dimension 0
- grad_w_gate: bfloat16 [32, 2048, 384], P(('group', 'owner')), parts along dimension 0
- grad_w_up: bfloat16 [32, 2048, 384], P(('group', 'owner')), parts along dimension 0
- grad_w_down: bfloat16 [32, 384, 2048], P(('group', 'owner')), parts along dimension 0
The draws below stay inside these ranges and needn't reach their ends.
There are 2 independent parts, one for each index of `group`. The reference program is written for one: setup_inputs(seed, part) draws one part's arguments, and reference() takes and returns one part's arrays. A program takes and returns all parts, laid end to end along the dimension named above; an argument that names none is the same for every part. Nothing has to cross between parts.
Inputs may be any that keep to these rules, and one draw needn't show every extreme that they name: `route_ids`: each token names 3 different experts. The 128 tokens of one owner device (aligned blocks) name any one expert at most 48 times, and some expert exactly 48 times.
All inputs are finite; a program needn't handle non-finite values.
Results may differ from the reference program's by a relative error of at most 0.008.
Values may be sent and summed in bfloat16 or wider, within the bound.
No kernel may reach another device: no remote copies, remote signals or barrier semaphores. Data moves between devices by JAX's collectives and lax.ppermute only.
A program may use at most 128 MiB of HBM per device.

```python
import math
import jax
import jax.numpy as jnp
from jax import lax

D = 2048
FFW = 384
TOK_DEV = 128
TOPW = 3
EXPERTS = 16
MOST = 48
TOKENS = 2048
N_OWNER = 16


def draw_route_ids(key, part):
    assign_block = TOK_DEV * TOPW
    block_count = TOKENS // TOK_DEV
    extra_count = (EXPERTS - 1) // 2
    cycle_length = EXPERTS - 1 + extra_count
    key_hot = jax.random.fold_in(key, 11)
    key_blocks = jax.random.fold_in(key, 23)
    hot_id = jax.random.randint(key_hot, (), 0, EXPERTS).astype(jnp.int32)

    def one_block(block_key):
        key_order = jax.random.fold_in(block_key, 1)
        key_tokens = jax.random.fold_in(block_key, 2)
        others = jax.random.permutation(key_order, EXPERTS - 1).astype(jnp.int32)
        others = others + (others >= hot_id).astype(jnp.int32)
        cycle = jnp.concatenate([others, others[:extra_count]])
        position = jnp.arange(assign_block, dtype=jnp.int32)
        rest = cycle[jnp.maximum(position - MOST, 0) % cycle_length]
        labels = jnp.where(position < MOST, hot_id, rest)
        runs = jnp.sort(labels)
        table = runs.reshape(TOPW, TOK_DEV).T
        token_order = jax.random.permutation(key_tokens, TOK_DEV)
        return table[token_order]
    block_keys = jax.random.split(key_blocks, block_count)
    blocks = jax.vmap(one_block)(block_keys)
    return blocks.reshape(TOKENS, TOPW).astype(jnp.int32)


def shard_levels(stream_key, extent, pieces, smallest, largest):
    loudness = 1.0
    for axis_at, blocks in pieces:
        heights = jax.random.uniform(jax.random.fold_in(jax.random.fold_in(stream_key, 6), axis_at), (blocks,), jnp.float32, smallest / len(pieces), largest / len(pieces))
        loudness = loudness * jnp.repeat(jnp.exp(heights), extent[axis_at] // blocks).reshape((-1,) + (1,) * (len(extent) - 1 - axis_at))
    return loudness


def noise(stream_key, dims, scale, reach, shards=(), kind=jnp.bfloat16):
    result = jax.random.normal(stream_key, dims, jnp.float32) * scale
    if len(shards) > 0:
        result = shard_levels(stream_key, dims, shards, -0.22, 0.18) * result
    return jnp.clip(result, min=-reach, max=reach).astype(kind)


def setup_inputs(seed: int = 0, part: int = 0) -> dict:
    splits = jax.random.split(jax.random.key(seed), 8)
    own_keys = jax.random.split(jax.random.fold_in(splits[7], part), 8)
    return {
        "tokens": noise(own_keys[0], (TOKENS, D), 1.0, 6.0, ((0, 16),)),
        "cotangent": noise(own_keys[1], (TOKENS, D), 1.0, 6.0, ((0, 16),)),
        "route_ids": draw_route_ids(jax.random.fold_in(jax.random.fold_in(splits[7], part), 71), part),
        "gate_probs": jnp.clip(jnp.exp(math.log(1.0) - 2.9957323 * jax.random.uniform(own_keys[3], (TOKENS, TOPW), jnp.float32) ** shard_levels(own_keys[3], (TOKENS, TOPW), ((0, 16),), -0.2, 0.2)), 0.05, 1.0),
        "w_gate": noise(splits[4], (EXPERTS, D, FFW), D ** -0.5, 0.125, ((0, 16),)),
        "w_up": noise(splits[5], (EXPERTS, D, FFW), D ** -0.5, 0.125, ((0, 16),)),
        "w_down": noise(splits[6], (EXPERTS, FFW, D), FFW ** -0.5, 0.3125, ((0, 16),)),
    }


def expert_pass(tokens_in, cotan_in, gate_w, up_w, down_w):
    gate_pre = jnp.dot(tokens_in, gate_w, preferred_element_type=jnp.float32)
    up_pre = jnp.dot(tokens_in, up_w, preferred_element_type=jnp.float32)
    gate_sig = jax.nn.sigmoid(gate_pre)
    gate_act = gate_pre * gate_sig
    hidden = (gate_act * up_pre).astype(jnp.bfloat16)
    expert_y = jnp.dot(hidden, down_w, preferred_element_type=jnp.float32).astype(jnp.bfloat16)
    d_hidden = jnp.dot(cotan_in, down_w.T, preferred_element_type=jnp.float32)
    grad_gate_pre = (d_hidden * up_pre * gate_sig * (1.0 + gate_pre * (1.0 - gate_sig))).astype(jnp.bfloat16)
    grad_up_pre = (d_hidden * gate_act).astype(jnp.bfloat16)
    expert_dx = (jnp.dot(grad_gate_pre, gate_w.T, preferred_element_type=jnp.float32)
                 + jnp.dot(grad_up_pre, up_w.T, preferred_element_type=jnp.float32)).astype(jnp.bfloat16)
    return expert_y, expert_dx, hidden, grad_gate_pre, grad_up_pre


def reference(tokens, cotangent, route_ids, gate_probs, w_gate, w_up, w_down):
    assign_count = TOKENS * TOPW
    capacity = MOST * N_OWNER
    flat_ids = route_ids.reshape(assign_count)
    zero_row = jnp.zeros((1, D), jnp.bfloat16)
    token_copies = jnp.concatenate([jnp.repeat(tokens, TOPW, axis=0), zero_row], axis=0)
    scaled_cot = (gate_probs[:, :, None] * cotangent[:, None, :].astype(jnp.float32)).astype(jnp.bfloat16)
    cotan_ext = jnp.concatenate([scaled_cot.reshape(assign_count, D), zero_row], axis=0)

    def per_expert(carried, expert):
        out_rows, back_rows = carried
        picked = jnp.nonzero(flat_ids == expert, size=capacity, fill_value=assign_count)[0].astype(jnp.int32)
        rows_in = token_copies[picked]
        cotan_in = cotan_ext[picked]
        expert_y, expert_dx, hidden, grad_gate_pre, grad_up_pre = expert_pass(
            rows_in, cotan_in, w_gate[expert], w_up[expert], w_down[expert])
        grad_gate = jnp.dot(rows_in.T, grad_gate_pre, preferred_element_type=jnp.float32).astype(jnp.bfloat16)
        grad_up = jnp.dot(rows_in.T, grad_up_pre, preferred_element_type=jnp.float32).astype(jnp.bfloat16)
        grad_down = jnp.dot(hidden.T, cotan_in, preferred_element_type=jnp.float32).astype(jnp.bfloat16)
        out_rows = out_rows.at[picked].set(expert_y, mode="drop")
        back_rows = back_rows.at[picked].set(expert_dx, mode="drop")
        return (out_rows, back_rows), (grad_gate, grad_up, grad_down)

    initial = (jnp.zeros((assign_count, D), jnp.bfloat16), jnp.zeros((assign_count, D), jnp.bfloat16))
    (out_rows, back_rows), (grad_w_gate, grad_w_up, grad_w_down) = lax.scan(
        per_expert, initial, jnp.arange(EXPERTS, dtype=jnp.int32))
    routed_y = out_rows.reshape(TOKENS, TOPW, D).astype(jnp.float32)
    expert_out = jnp.sum(gate_probs[:, :, None] * routed_y, axis=1).astype(jnp.bfloat16)
    grad_tokens = jnp.sum(back_rows.reshape(TOKENS, TOPW, D).astype(jnp.float32), axis=1).astype(jnp.bfloat16)
    grad_gates = jnp.sum(routed_y * cotangent[:, None, :].astype(jnp.float32), axis=2)
    return expert_out, grad_tokens, grad_gates, grad_w_gate, grad_w_up, grad_w_down
```

```python
import jax
import jax.numpy as jnp
from jax import lax
from jax.sharding import PartitionSpec as P

F32 = jnp.float32
BF16 = jnp.bfloat16
LANES = 128


def rounded(value):
    return lax.reduce_precision(value, exponent_bits=8, mantissa_bits=7)


def split_three(value):
    high = rounded(value)
    rest = value - high
    middle = rounded(rest)
    low = rounded(rest - middle)
    return high, middle, low


def expert_pass(rows_x, rows_c, gate_w, up_w, down_w):
    def fwd(a, w):
        return jnp.einsum("erd,edf->erf", a, w, preferred_element_type=F32)

    def bwd(a, w):
        return jnp.einsum("erf,edf->erd", a, w, preferred_element_type=F32)

    gate_pre = fwd(rows_x, gate_w)
    up_pre = fwd(rows_x, up_w)
    gate_sig = jax.nn.sigmoid(gate_pre)
    gate_act = gate_pre * gate_sig
    hidden = (gate_act * up_pre).astype(BF16)
    expert_y = fwd(hidden, down_w).astype(BF16)
    d_hidden = bwd(rows_c, down_w)
    grad_gate_pre = (d_hidden * up_pre * gate_sig * (1.0 + gate_pre * (1.0 - gate_sig))).astype(BF16)
    grad_up_pre = (d_hidden * gate_act).astype(BF16)
    expert_dx = (bwd(grad_gate_pre, gate_w) + bwd(grad_up_pre, up_w)).astype(BF16)
    return expert_y, expert_dx, hidden, grad_gate_pre, grad_up_pre


def local(tokens, cotangent, route_ids, gate_probs, w_gate, w_up, w_down):
    owner_count = lax.axis_size("owner")
    me = lax.axis_index("owner")
    token_rows, width = tokens.shape
    route_count = route_ids.shape[1]
    depth = 2 * token_rows * route_count // owner_count
    side = 2 if owner_count % 4 == 0 else 1
    plane = 2 * side
    ring = owner_count // plane
    core = me % 2
    column = me % plane
    my_z = me // plane
    chip_slots = 2 * depth

    ring_up = [(i, (i + plane) % owner_count) for i in range(owner_count)]
    across = [(i, i ^ 2) for i in range(owner_count)]
    partner = [(i, i ^ 1) for i in range(owner_count)]

    def hop(value, pairs):
        return lax.ppermute(value, "owner", pairs)

    both_gate = jnp.stack([w_gate[0], hop(w_gate[0], partner)])
    both_up = jnp.stack([w_up[0], hop(w_up[0], partner)])
    both_down = jnp.stack([w_down[0], hop(w_down[0], partner)])

    offsets = jnp.arange(plane, dtype=jnp.int32)
    plane_experts = my_z * plane + jnp.bitwise_xor(column, (offsets // 2) * 2 + offsets % 2)

    id_table = route_ids.reshape(ring, plane, token_rows, route_count)
    line_ids = lax.dynamic_index_in_dim(id_table, column, 1, keepdims=False)
    slot_range = jnp.arange(depth, dtype=jnp.int32)

    p_parts = jnp.concatenate(split_three(gate_probs), axis=1).astype(BF16)
    pad = jnp.zeros((token_rows, LANES - p_parts.shape[1]), BF16)
    block = jnp.concatenate([tokens, cotangent, p_parts, pad], axis=1)

    blocks = [block]
    for _ in range(ring - 1):
        blocks.append(hop(blocks[-1], ring_up))

    def prepare(step):
        ids = lax.dynamic_index_in_dim(line_ids, (my_z - step) % ring, 0, keepdims=False)
        data = blocks[step]
        parts = data[:, 2 * width : 2 * width + 3 * route_count].astype(F32)
        probs = (
            parts[:, :route_count]
            + parts[:, route_count : 2 * route_count]
            + parts[:, 2 * route_count :]
        )
        match = ids[None, :, :] == plane_experts[:, None, None]
        named = jnp.any(match, axis=2)
        rank = jnp.cumsum(named.astype(jnp.int32), axis=1) - 1
        pick = named[:, None, :] & (rank[:, None, :] == slot_range[None, :, None])
        prob = jnp.sum(jnp.where(match, probs[None], 0.0), axis=2)
        slot_prob = jnp.sum(jnp.where(pick, prob[:, None, :], 0.0), axis=2)
        pick_flat = pick.reshape(plane * depth, token_rows)
        return ids, data, match, pick_flat, slot_prob.reshape(plane * depth)

    rows_x, rows_c, packs = [], [], []
    for step in range(ring):
        ids, data, match, pick, slot_prob = prepare(step)
        chooser = pick.astype(BF16)
        sel_x = jnp.dot(chooser, data[:, :width], preferred_element_type=F32).astype(BF16)
        sel_c = jnp.dot(chooser, data[:, width : 2 * width], preferred_element_type=F32)
        sel_c = (sel_c * slot_prob[:, None]).astype(BF16)
        own_x = sel_x[:chip_slots].reshape(2, depth, width)
        own_c = sel_c[:chip_slots].reshape(2, depth, width)
        if side == 2:
            sent = jnp.concatenate([sel_x[chip_slots:], sel_c[chip_slots:]], axis=1)
            got = hop(sent, across).reshape(2, depth, 2 * width)
            own_x = jnp.concatenate([own_x, got[:, :, :width]], axis=1)
            own_c = jnp.concatenate([own_c, got[:, :, width:]], axis=1)
        rows_x.append(own_x)
        rows_c.append(own_c)
        packs.append((data, match, pick, slot_prob))

    results = [
        expert_pass(rows_x[step], rows_c[step], both_gate, both_up, both_down)
        for step in range(ring)
    ]

    def combine(step):
        data, match, pick, slot_prob = packs[step]
        out_y, out_dx = results[step][:2]
        near_y = out_y[:, :depth].reshape(chip_slots, width)
        near_dx = out_dx[:, :depth].reshape(chip_slots, width)
        if side == 2:
            sent = jnp.concatenate([out_y[:, depth:], out_dx[:, depth:]], axis=2)
            got = hop(sent.reshape(chip_slots, 2 * width), across)
            near_y = jnp.concatenate([near_y, got[:, :width]], axis=0)
            near_dx = jnp.concatenate([near_dx, got[:, width:]], axis=0)
        spread = pick.T
        weight = jnp.where(spread, slot_prob[None, :], 0.0)
        weight_high = rounded(weight)
        weight_low = (weight - weight_high).astype(BF16)
        part_y = jnp.dot(
            weight_high.astype(BF16), near_y, preferred_element_type=F32
        ) + jnp.dot(weight_low, near_y, preferred_element_type=F32)
        part_dx = jnp.dot(spread.astype(BF16), near_dx, preferred_element_type=F32)
        dots = lax.dot_general(
            data[:, width : 2 * width],
            near_y,
            (((1,), (1,)), ((), ())),
            preferred_element_type=F32,
        )
        per_expert = jnp.sum(
            jnp.where(spread, dots, 0.0).reshape(token_rows, plane, depth), axis=2
        )
        part_gates = jnp.sum(jnp.where(match, per_expert.T[:, :, None], 0.0), axis=0)
        return part_y, part_dx, part_gates

    def pack_out(part_y, part_dx, part_gates):
        gates = jnp.concatenate(split_three(part_gates), axis=1)
        return jnp.concatenate(
            [part_y.astype(BF16), part_dx.astype(BF16), gates.astype(BF16), pad], axis=1
        )

    def unpack(value):
        value = value.astype(F32)
        gates = value[:, 2 * width : 2 * width + 3 * route_count]
        gates = gates.reshape(token_rows, 3, route_count).sum(axis=1)
        return value[:, :width], value[:, width : 2 * width], gates

    running = None
    for step in list(range(1, ring)) + [0]:
        part = combine(step)
        if running is not None:
            part = tuple(a + b for a, b in zip(part, unpack(running)))
        if step != 0:
            running = hop(pack_out(*part), ring_up)
    expert_out, grad_tokens, grad_gates = part

    all_x = jnp.concatenate(rows_x, axis=1)
    all_c = jnp.concatenate(rows_c, axis=1)
    hidden = jnp.concatenate([r[2] for r in results], axis=1)
    grad_gate_pre = jnp.concatenate([r[3] for r in results], axis=1)
    grad_up_pre = jnp.concatenate([r[4] for r in results], axis=1)

    def outer(a, b, which):
        return jnp.einsum("rm,rn->mn", a[which], b[which], preferred_element_type=F32)

    outs = []
    for left, right in ((all_x, grad_gate_pre), (all_x, grad_up_pre), (hidden, all_c)):
        theirs = outer(left, right, 1).astype(BF16)
        mine = outer(left, right, 0)
        outs.append((mine + hop(theirs, partner).astype(F32)).astype(BF16)[None])

    return (
        expert_out.astype(BF16),
        grad_tokens.astype(BF16),
        grad_gates,
        outs[0],
        outs[1],
        outs[2],
    )


def solution(mesh):
    rows = P(("group", "owner"), None)
    stacked = P(("group", "owner"), None, None)
    weights = P("owner", None, None)
    return jax.shard_map(
        local,
        mesh=mesh,
        in_specs=(rows, rows, P("group", None), rows, weights, weights, weights),
        out_specs=(rows, rows, rows, stacked, stacked, stacked),
        check_vma=False,
    )
```

```python
import functools

import jax
import jax.numpy as jnp
from jax import lax
from jax.experimental import pallas as pl
from jax.experimental.pallas import tpu as pltpu
from jax.sharding import PartitionSpec as P

F32 = jnp.float32
BF16 = jnp.bfloat16
LANES = 128
TILE = 512
VMEM = pl.BlockSpec(memory_space=pltpu.VMEM)
SMEM = pl.BlockSpec(memory_space=pltpu.SMEM)


def rounded(value):
    return value.astype(BF16).astype(F32)


def nt(a, b):
    return lax.dot_general(a, b, (((1,), (1,)), ((), ())), preferred_element_type=F32)


def nn(a, b):
    return jnp.dot(a, b, preferred_element_type=F32)


def expert_ids(place, plane):
    return [place[0] * plane + jnp.bitwise_xor(place[1], e) for e in range(plane)]


def slots_of(place, ids, parts, plane, depth, route_count):
    tokens = ids.shape[1]
    rows = lax.broadcasted_iota(jnp.int32, (tokens, tokens), 0)
    cols = lax.broadcasted_iota(jnp.int32, (tokens, tokens), 1)
    before = jnp.where(rows < cols, 1.0, 0.0).astype(BF16)
    route = [ids[k : k + 1] for k in range(route_count)]
    probs = [
        parts[k : k + 1]
        + parts[route_count + k : route_count + k + 1]
        + parts[2 * route_count + k : 2 * route_count + k + 1]
        for k in range(route_count)
    ]
    slot = lax.broadcasted_iota(jnp.int32, (depth, tokens), 0)
    named, weight = [], []
    for eid in expert_ids(place, plane):
        hit = [jnp.where(r == eid, 1.0, 0.0) for r in route]
        named.append(sum(hit))
        weight.append(sum(h * p for h, p in zip(hit, probs)))
    pad = [jnp.zeros((8 - plane % 8, tokens), F32)] if plane % 8 else []
    rank = nn(jnp.concatenate(named + pad, axis=0).astype(BF16), before)
    picks, gates = [], []
    for e in range(plane):
        wanted = jnp.broadcast_to(rank[e : e + 1], (depth, tokens)).astype(jnp.int32)
        present = jnp.broadcast_to(named[e], (depth, tokens))
        pick = jnp.where(wanted == slot, present, 0.0)
        picks.append(pick)
        gates.append(jnp.sum(pick * weight[e], axis=1, keepdims=True))
    return jnp.concatenate(picks, axis=0), jnp.concatenate(gates, axis=0)


def select_kernel(plane, depth, route_count, place, ids, block, *outs):
    width = outs[0].shape[1] // 2
    parts = block[0:16, 2 * width :].astype(F32)
    pick, gate = slots_of(place, ids[...], parts, plane, depth, route_count)
    chooser = pick.astype(BF16)
    for start in range(0, 2 * width, TILE):
        cols = pl.ds(start, TILE)
        found = nn(chooser, block[:, cols])
        if start >= width:
            found = found * gate
        found = found.astype(BF16)
        for e in range(plane):
            outs[e][:, cols] = found[e * depth : (e + 1) * depth]


def expert_kernel(plane, *refs):
    rows = refs[:plane]
    gate_w, up_w, down_w = refs[plane : plane + 3]
    outs = refs[plane + 3 : 2 * plane + 3]
    hidden_out, ggp_out, gup_out = refs[2 * plane + 3 :]
    width = gate_w.shape[0]
    depth = rows[0].shape[0]
    row_x = jnp.concatenate([r[:, :width] for r in rows], axis=0)
    row_c = jnp.concatenate([r[:, width:] for r in rows], axis=0)
    gate_pre = nn(row_x, gate_w[...])
    up_pre = nn(row_x, up_w[...])
    gate_sig = 1.0 / (1.0 + jnp.exp(-gate_pre))
    gate_act = gate_pre * gate_sig
    hidden = (gate_act * up_pre).astype(BF16)
    hidden_out[...] = hidden
    d_hidden = nt(row_c, down_w[...])
    ggp = (d_hidden * up_pre * gate_sig * (1.0 + gate_pre * (1.0 - gate_sig))).astype(BF16)
    gup = (d_hidden * gate_act).astype(BF16)
    ggp_out[...] = ggp
    gup_out[...] = gup
    for start in range(0, width, TILE):
        cols = pl.ds(start, TILE)
        y = nn(hidden, down_w[:, cols]).astype(BF16)
        dx = (nt(ggp, gate_w[cols, :]) + nt(gup, up_w[cols, :])).astype(BF16)
        for e in range(plane):
            part = slice(e * depth, (e + 1) * depth)
            outs[e][:, cols] = y[part]
            outs[e][:, pl.ds(width + start, TILE)] = dx[part]


def combine_kernel(plane, depth, route_count, has_running, is_last, place, ids, block, *refs):
    near = refs[:plane]
    refs = refs[plane:]
    running = None
    if has_running:
        running, refs = refs[0], refs[1:]
    width = near[0].shape[1] // 2
    tokens = ids.shape[1]
    ids_now = ids[...]
    parts = block[0:16, 2 * width :].astype(F32)
    pick, gate = slots_of(place, ids_now, parts, plane, depth, route_count)
    weighted = pick * gate
    weight_high = rounded(weighted)
    high = jnp.transpose(weight_high).astype(BF16)
    low = jnp.transpose(weighted - weight_high).astype(BF16)
    spread = jnp.transpose(pick).astype(BF16)
    dots = jnp.zeros((plane * depth, tokens), F32)
    for start in range(0, width, TILE):
        cols = pl.ds(start, TILE)
        cols_dx = pl.ds(width + start, TILE)
        y = jnp.concatenate([n[:, cols] for n in near], axis=0)
        dx = jnp.concatenate([n[:, cols_dx] for n in near], axis=0)
        part_y = nn(high, y) + nn(low, y)
        part_dx = nn(spread, dx)
        dots = dots + nt(y, block[:, cols_dx])
        if has_running:
            part_y = part_y + running[:, cols].astype(F32)
            part_dx = part_dx + running[:, cols_dx].astype(F32)
        if is_last:
            refs[0][:, cols] = part_y.astype(BF16)
            refs[1][:, cols] = part_dx.astype(BF16)
        else:
            refs[0][:, cols] = part_y.astype(BF16)
            refs[0][:, cols_dx] = part_dx.astype(BF16)
    dots = pick * dots
    found = [jnp.sum(dots[e * depth : (e + 1) * depth], axis=0, keepdims=True) for e in range(plane)]
    gates = []
    for k in range(route_count):
        mine = ids_now[k : k + 1]
        total = jnp.zeros((1, tokens), F32)
        for eid, value in zip(expert_ids(place, plane), found):
            total = total + jnp.where(mine == eid, value, 0.0)
        gates.append(total)
    if has_running:
        old = running[0:16, 2 * width :].astype(F32)
        for k in range(route_count):
            for piece in range(3):
                at = piece * route_count + k
                gates[k] = gates[k] + old[at : at + 1]
    if is_last:
        pad = jnp.zeros((8 - route_count, tokens), F32)
        refs[2][...] = jnp.concatenate(gates + [pad], axis=0)
    else:
        high = [rounded(g) for g in gates]
        middle = [rounded(g - h) for g, h in zip(gates, high)]
        low = [g - h - m for g, h, m in zip(gates, high, middle)]
        pad = jnp.zeros((tokens - 3 * route_count, tokens), F32)
        refs[0][:, 2 * width :] = jnp.concatenate(high + middle + low + [pad], axis=0).astype(BF16)


def grads_kernel(ring, plane, *refs):
    rows = refs[: ring * plane]
    small = refs[ring * plane : ring * plane + 3 * ring]
    gate_out, up_out, down_out = refs[ring * plane + 3 * ring :]
    width = gate_out.shape[0]
    hidden = jnp.transpose(jnp.concatenate([small[3 * s][...] for s in range(ring)], axis=0))
    ggp = jnp.concatenate([small[3 * s + 1][...] for s in range(ring)], axis=0)
    gup = jnp.concatenate([small[3 * s + 2][...] for s in range(ring)], axis=0)
    step = TILE // 2
    for start in range(0, width, step):
        cols = pl.ds(start, step)
        x = jnp.transpose(jnp.concatenate([r[:, cols] for r in rows], axis=0))
        gate_out[cols, :] = nn(x, ggp).astype(BF16)
        up_out[cols, :] = nn(x, gup).astype(BF16)
        c = jnp.concatenate([r[:, pl.ds(width + start, step)] for r in rows], axis=0)
        down_out[:, cols] = nn(hidden, c).astype(BF16)


def call(body, outs, flops, inputs, name):
    total = sum(x.size * x.dtype.itemsize for x in inputs)
    total += sum(o.size * o.dtype.itemsize for o in outs)
    specs = [SMEM if x.dtype == jnp.int32 and x.ndim == 1 else VMEM for x in inputs]
    return pl.pallas_call(
        body,
        out_shape=tuple(outs),
        in_specs=specs,
        out_specs=tuple(VMEM for _ in outs),
        cost_estimate=pl.CostEstimate(flops=flops, bytes_accessed=total, transcendentals=0),
        compiler_params=pltpu.CompilerParams(vmem_limit_bytes=40 * 1024 * 1024),
        name=name,
    )(*inputs)


def local(tokens, cotangent, route_ids, gate_probs, w_gate, w_up, w_down):
    owner_count = lax.axis_size("owner")
    me = lax.axis_index("owner")
    token_rows, width = tokens.shape
    route_count = route_ids.shape[1]
    hidden_width = w_gate.shape[2]
    depth = 2 * token_rows * route_count // owner_count
    depth = (depth + 15) // 16 * 16
    plane = 4 if owner_count % 4 == 0 else 2
    ring = owner_count // plane
    column = me % plane
    my_z = me // plane
    place = jnp.stack([my_z, column]).astype(jnp.int32)

    ring_up = [(i, (i + plane) % owner_count) for i in range(owner_count)]
    swaps = [[(i, i ^ e) for i in range(owner_count)] for e in range(plane)]

    def hop(value, pairs, scope):
        with jax.named_scope(scope):
            return lax.ppermute(value, "owner", pairs)

    id_table = route_ids.reshape(ring, plane, token_rows, route_count)
    line_ids = lax.dynamic_index_in_dim(id_table, column, 1, keepdims=False)
    line_ids = jnp.swapaxes(line_ids, 1, 2)
    line_ids = jnp.pad(line_ids, ((0, 0), (0, 8 - route_count), (0, 0)), constant_values=-1)
    step_ids = [
        lax.dynamic_index_in_dim(line_ids, (my_z - s) % ring, 0, keepdims=False) for s in range(ring)
    ]

    probs = gate_probs.T
    high = lax.reduce_precision(probs, 8, 7)
    middle = lax.reduce_precision(probs - high, 8, 7)
    low = probs - high - middle
    tail = jnp.concatenate([high, middle, low], axis=0).astype(BF16)
    tail = jnp.pad(tail, ((0, token_rows - 3 * route_count), (0, 0)))
    block = jnp.concatenate([tokens, cotangent, tail], axis=1)
    packed = 2 * width + token_rows

    blocks = [block]
    for s in range(ring - 1):
        blocks.append(hop(blocks[-1], ring_up, f"zin{s + 1}"))

    slot_shape = jax.ShapeDtypeStruct((depth, 2 * width), BF16)
    small_shape = jax.ShapeDtypeStruct((plane * depth, hidden_width), BF16)
    weights = [w_gate[0], w_up[0], w_down[0]]
    rows = plane * depth

    def exchange(values, scope):
        return [values[0]] + [hop(values[e], swaps[e], f"{scope}_{e}") for e in range(1, plane)]

    got, result = [], []
    for s in range(ring):
        picked = call(
            functools.partial(select_kernel, plane, depth, route_count),
            [slot_shape] * plane,
            2 * rows * token_rows * 2 * width,
            [place, step_ids[s], blocks[s]],
            f"select{s}",
        )
        got.append(exchange(picked, f"yin{s}"))
    for s in range(ring):
        result.append(
            call(
                functools.partial(expert_kernel, plane),
                [slot_shape] * plane + [small_shape] * 3,
                12 * rows * width * hidden_width,
                got[s] + weights,
                f"expert{s}",
            )
        )

    running = None
    for s in list(range(1, ring)) + [0]:
        near = exchange(result[s][:plane], f"yout{s}")
        last = s == 0
        if last:
            row_shape = jax.ShapeDtypeStruct((token_rows, width), BF16)
            outs = [row_shape, row_shape, jax.ShapeDtypeStruct((8, token_rows), F32)]
        else:
            outs = [jax.ShapeDtypeStruct((token_rows, packed), BF16)]
        inputs = [place, step_ids[s], blocks[s]] + near
        if running is not None:
            inputs.append(running)
        done = call(
            functools.partial(
                combine_kernel, plane, depth, route_count, running is not None, last
            ),
            outs,
            8 * rows * token_rows * width,
            inputs,
            f"combine{s}",
        )
        if not last:
            running = hop(done[0], ring_up, f"zout{s}")
    expert_out, grad_tokens, gates = done

    small = [r for s in range(ring) for r in result[s][plane:]]
    grads = call(
        functools.partial(grads_kernel, ring, plane),
        [
            jax.ShapeDtypeStruct((width, hidden_width), BF16),
            jax.ShapeDtypeStruct((width, hidden_width), BF16),
            jax.ShapeDtypeStruct((hidden_width, width), BF16),
        ],
        6 * ring * rows * width * hidden_width,
        [g for s in range(ring) for g in got[s]] + small,
        "grads",
    )
    return (
        expert_out,
        grad_tokens,
        gates[:route_count].T,
        grads[0][None],
        grads[1][None],
        grads[2][None],
    )


def solution(mesh):
    rows = P(("group", "owner"), None)
    stacked = P(("group", "owner"), None, None)
    weights = P("owner", None, None)
    return jax.shard_map(
        local,
        mesh=mesh,
        in_specs=(rows, rows, P("group", None), rows, weights, weights, weights),
        out_specs=(rows, rows, rows, stacked, stacked, stacked),
        check_vma=False,
    )
```

```python
import functools

import jax
import jax.numpy as jnp
from jax import lax
from jax.experimental import pallas as pl
from jax.experimental.pallas import tpu as pltpu
from jax.sharding import PartitionSpec as P


F32 = jnp.float32
BF16 = jnp.bfloat16
TILE = 512
VMEM = pl.BlockSpec(memory_space=pltpu.VMEM)
SMEM = pl.BlockSpec(memory_space=pltpu.SMEM)


def rounded(value):
    return value.astype(BF16).astype(F32)


def nt(a, b):
    return lax.dot_general(a, b, (((1,), (1,)), ((), ())), preferred_element_type=F32)


def nn(a, b):
    return jnp.dot(a, b, preferred_element_type=F32)


def expert_ids(place, plane):
    return [place[0] * plane + jnp.bitwise_xor(place[1], e) for e in range(plane)]


def slots_of(place, ids, parts, plane, depth, route_count):
    tokens = ids.shape[1]
    rows = lax.broadcasted_iota(jnp.int32, (tokens, tokens), 0)
    cols = lax.broadcasted_iota(jnp.int32, (tokens, tokens), 1)
    before = jnp.where(rows < cols, 1.0, 0.0).astype(BF16)
    route = [ids[k : k + 1] for k in range(route_count)]
    probs = [
        parts[k : k + 1]
        + parts[route_count + k : route_count + k + 1]
        + parts[2 * route_count + k : 2 * route_count + k + 1]
        for k in range(route_count)
    ]
    slot = lax.broadcasted_iota(jnp.int32, (depth, tokens), 0)
    named, weight = [], []
    for eid in expert_ids(place, plane):
        hit = [jnp.where(r == eid, 1.0, 0.0) for r in route]
        named.append(sum(hit))
        weight.append(sum(h * p for h, p in zip(hit, probs)))
    pad = [jnp.zeros((8 - plane % 8, tokens), F32)] if plane % 8 else []
    rank = nn(jnp.concatenate(named + pad, axis=0).astype(BF16), before)
    picks, gates = [], []
    for e in range(plane):
        wanted = jnp.broadcast_to(rank[e : e + 1], (depth, tokens)).astype(jnp.int32)
        present = jnp.broadcast_to(named[e], (depth, tokens))
        pick = jnp.where(wanted == slot, present, 0.0)
        picks.append(pick)
        gates.append(jnp.sum(pick * weight[e], axis=1, keepdims=True))
    return jnp.concatenate(picks, axis=0), jnp.concatenate(gates, axis=0)


def select_kernel(plane, depth, route_count, scaled, place, ids, block, *outs):
    width = outs[0].shape[1]
    tokens = ids.shape[1]
    if scaled:
        parts = block[0:16, width:].astype(F32)
    else:
        parts = jnp.zeros((16, tokens), F32)
    pick, gate = slots_of(place, ids[...], parts, plane, depth, route_count)
    chooser = pick.astype(BF16)
    for start in range(0, width, TILE):
        cols = pl.ds(start, TILE)
        found = nn(chooser, block[:, cols])
        if scaled:
            found = found * gate
        found = found.astype(BF16)
        for e in range(plane):
            outs[e][:, cols] = found[e * depth : (e + 1) * depth]


def forward_kernel(plane, *refs):
    rows = refs[:plane]
    gate_w, up_w, down_w = refs[plane : plane + 3]
    outs = refs[plane + 3 : 2 * plane + 3]
    hidden_out, gate_out, up_out = refs[2 * plane + 3 :]
    width = gate_w.shape[0]
    depth = rows[0].shape[0]
    row_x = jnp.concatenate([r[...] for r in rows], axis=0)
    gate_pre = nn(row_x, gate_w[...])
    up_pre = nn(row_x, up_w[...])
    gate_out[...] = gate_pre
    up_out[...] = up_pre
    gate_sig = 1.0 / (1.0 + jnp.exp(-gate_pre))
    hidden = (gate_pre * gate_sig * up_pre).astype(BF16)
    hidden_out[...] = hidden
    for start in range(0, width, TILE):
        cols = pl.ds(start, TILE)
        y = nn(hidden, down_w[:, cols]).astype(BF16)
        for e in range(plane):
            outs[e][:, cols] = y[e * depth : (e + 1) * depth]


def backward_kernel(plane, *refs):
    rows = refs[:plane]
    gate_pre, up_pre, gate_w, up_w, down_w = refs[plane : plane + 5]
    outs = refs[plane + 5 : 2 * plane + 5]
    ggp_out, gup_out = refs[2 * plane + 5 :]
    width = gate_w.shape[0]
    depth = rows[0].shape[0]
    row_c = jnp.concatenate([r[...] for r in rows], axis=0)
    d_hidden = nt(row_c, down_w[...])
    gate_pre = gate_pre[...]
    gate_sig = 1.0 / (1.0 + jnp.exp(-gate_pre))
    slope = gate_sig * (1.0 + gate_pre * (1.0 - gate_sig))
    ggp = (d_hidden * up_pre[...] * slope).astype(BF16)
    gup = (d_hidden * (gate_pre * gate_sig)).astype(BF16)
    ggp_out[...] = ggp
    gup_out[...] = gup
    for start in range(0, width, TILE):
        cols = pl.ds(start, TILE)
        dx = (nt(ggp, gate_w[cols, :]) + nt(gup, up_w[cols, :])).astype(BF16)
        for e in range(plane):
            outs[e][:, cols] = dx[e * depth : (e + 1) * depth]


def combine_out_kernel(plane, depth, route_count, has_running, is_last, place, ids, block, *refs):
    near = refs[:plane]
    refs = refs[plane:]
    running = None
    if has_running:
        running, refs = refs[0], refs[1:]
    width = near[0].shape[1]
    tokens = ids.shape[1]
    ids_now = ids[...]
    parts = block[0:16, width:].astype(F32)
    pick, gate = slots_of(place, ids_now, parts, plane, depth, route_count)
    weighted = pick * gate
    weight_high = rounded(weighted)
    high = jnp.transpose(weight_high).astype(BF16)
    low = jnp.transpose(weighted - weight_high).astype(BF16)
    dots = jnp.zeros((plane * depth, tokens), F32)
    for start in range(0, width, TILE):
        cols = pl.ds(start, TILE)
        y = jnp.concatenate([n[:, cols] for n in near], axis=0)
        part_y = nn(high, y) + nn(low, y)
        dots = dots + nt(y, block[:, cols])
        if has_running:
            part_y = part_y + running[:, cols].astype(F32)
        refs[0][:, cols] = part_y.astype(BF16)
    dots = pick * dots
    found = [jnp.sum(dots[e * depth : (e + 1) * depth], axis=0, keepdims=True) for e in range(plane)]
    gates = []
    for k in range(route_count):
        mine = ids_now[k : k + 1]
        total = jnp.zeros((1, tokens), F32)
        for eid, value in zip(expert_ids(place, plane), found):
            total = total + jnp.where(mine == eid, value, 0.0)
        gates.append(total)
    if has_running:
        old = running[0:16, width:].astype(F32)
        for k in range(route_count):
            for piece in range(3):
                at = piece * route_count + k
                gates[k] = gates[k] + old[at : at + 1]
    if is_last:
        pad = jnp.zeros((8 - route_count, tokens), F32)
        refs[1][...] = jnp.concatenate(gates + [pad], axis=0)
    else:
        high = [rounded(g) for g in gates]
        middle = [rounded(g - h) for g, h in zip(gates, high)]
        low = [g - h - m for g, h, m in zip(gates, high, middle)]
        pad = jnp.zeros((tokens - 3 * route_count, tokens), F32)
        refs[0][:, width:] = jnp.concatenate(high + middle + low + [pad], axis=0).astype(BF16)


def combine_back_kernel(plane, depth, route_count, has_running, place, ids, *refs):
    near = refs[:plane]
    out = refs[-1]
    width = near[0].shape[1]
    parts = jnp.zeros((16, ids.shape[1]), F32)
    pick, _ = slots_of(place, ids[...], parts, plane, depth, route_count)
    spread = jnp.transpose(pick).astype(BF16)
    for start in range(0, width, TILE):
        cols = pl.ds(start, TILE)
        dx = jnp.concatenate([n[:, cols] for n in near], axis=0)
        part_dx = nn(spread, dx)
        if has_running:
            part_dx = part_dx + refs[plane][:, cols].astype(F32)
        out[:, cols] = part_dx.astype(BF16)


def grads_kernel(ring, plane, *refs):
    count = ring * plane
    rows_x, rows_c = refs[:count], refs[count : 2 * count]
    small = refs[2 * count : 2 * count + 3 * ring]
    gate_out, up_out, down_out = refs[2 * count + 3 * ring :]
    width = gate_out.shape[0]
    hidden = jnp.transpose(jnp.concatenate([small[3 * s][...] for s in range(ring)], axis=0))
    ggp = jnp.concatenate([small[3 * s + 1][...] for s in range(ring)], axis=0)
    gup = jnp.concatenate([small[3 * s + 2][...] for s in range(ring)], axis=0)
    step = TILE // 2
    for start in range(0, width, step):
        cols = pl.ds(start, step)
        x = jnp.transpose(jnp.concatenate([r[:, cols] for r in rows_x], axis=0))
        gate_out[cols, :] = nn(x, ggp).astype(BF16)
        up_out[cols, :] = nn(x, gup).astype(BF16)
        c = jnp.concatenate([r[:, cols] for r in rows_c], axis=0)
        down_out[:, cols] = nn(hidden, c).astype(BF16)


def call(body, outs, flops, inputs):
    total = sum(x.size * x.dtype.itemsize for x in inputs)
    total += sum(o.size * o.dtype.itemsize for o in outs)
    specs = [SMEM if x.dtype == jnp.int32 and x.ndim == 1 else VMEM for x in inputs]
    return pl.pallas_call(
        body,
        out_shape=tuple(outs),
        in_specs=specs,
        out_specs=tuple(VMEM for _ in outs),
        cost_estimate=pl.CostEstimate(flops=flops, bytes_accessed=total, transcendentals=0),
        compiler_params=pltpu.CompilerParams(vmem_limit_bytes=40 * 1024 * 1024),
    )(*inputs)


def local(tokens, cotangent, route_ids, gate_probs, w_gate, w_up, w_down):
    owner_count = lax.axis_size("owner")
    me = lax.axis_index("owner")
    token_rows, width = tokens.shape
    route_count = route_ids.shape[1]
    hidden_width = w_gate.shape[2]
    depth = 2 * token_rows * route_count // owner_count
    depth = (depth + 15) // 16 * 16
    plane = 4 if owner_count % 4 == 0 else 2
    ring = owner_count // plane
    column = me % plane
    my_z = me // plane
    place = jnp.stack([my_z, column]).astype(jnp.int32)

    ring_up = [(i, (i + plane) % owner_count) for i in range(owner_count)]
    swaps = [[(i, i ^ e) for i in range(owner_count)] for e in range(plane)]

    def hop(value, pairs):
        return lax.ppermute(value, "owner", pairs)

    id_table = route_ids.reshape(ring, plane, token_rows, route_count)
    line_ids = lax.dynamic_index_in_dim(id_table, column, 1, keepdims=False)
    line_ids = jnp.swapaxes(line_ids, 1, 2)
    line_ids = jnp.pad(line_ids, ((0, 0), (0, 8 - route_count), (0, 0)), constant_values=-1)
    step_ids = [
        lax.dynamic_index_in_dim(line_ids, (my_z - s) % ring, 0, keepdims=False) for s in range(ring)
    ]

    probs = gate_probs.T
    high = lax.reduce_precision(probs, 8, 7)
    middle = lax.reduce_precision(probs - high, 8, 7)
    low = probs - high - middle
    tail = jnp.concatenate([high, middle, low], axis=0).astype(BF16)
    tail = jnp.pad(tail, ((0, token_rows - 3 * route_count), (0, 0)))
    block_x = [tokens]
    block_c = [jnp.concatenate([cotangent, tail], axis=1)]
    for _ in range(1, ring):
        block_x.append(hop(block_x[-1], ring_up))
        block_c.append(hop(block_c[-1], ring_up))

    def shape(*dims, kind=BF16):
        return jax.ShapeDtypeStruct(dims, kind)

    rows = plane * depth
    slots = [shape(depth, width)] * plane
    weights = [w_gate[0], w_up[0], w_down[0]]
    move_flops = 2 * rows * token_rows * width
    dense_flops = 2 * rows * width * hidden_width

    def exchange(values):
        return [values[0]] + [hop(values[e], swaps[e]) for e in range(1, plane)]

    got_x, got_c, small = [], [], []
    back_y, back_d = [], []
    for s in range(ring):
        for blocks, got, scaled in ((block_x, got_x, False), (block_c, got_c, True)):
            picked = call(
                functools.partial(select_kernel, plane, depth, route_count, scaled),
                slots,
                move_flops,
                [place, step_ids[s], blocks[s]],
            )
            got.append(exchange(picked))
        ahead = call(
            functools.partial(forward_kernel, plane),
            slots + [shape(rows, hidden_width)] + [shape(rows, hidden_width, kind=F32)] * 2,
            3 * dense_flops,
            got_x[s] + weights,
        )
        back = call(
            functools.partial(backward_kernel, plane),
            slots + [shape(rows, hidden_width)] * 2,
            3 * dense_flops,
            got_c[s] + list(ahead[plane + 1 :]) + weights,
        )
        small += [ahead[plane], back[plane], back[plane + 1]]
        back_y.append(exchange(ahead[:plane]))
        back_d.append(exchange(back[:plane]))

    run_y, run_d = [], []
    for s in list(range(1, ring)) + [0]:
        last = s == 0
        row = shape(token_rows, width)
        outs_y = [row, shape(8, token_rows, kind=F32)]
        if not last:
            outs_y = [shape(token_rows, width + token_rows)]
        done_y = call(
            functools.partial(
                combine_out_kernel, plane, depth, route_count, bool(run_y), last
            ),
            outs_y,
            3 * move_flops,
            [place, step_ids[s], block_c[s]] + back_y[s] + run_y,
        )
        done_d = call(
            functools.partial(combine_back_kernel, plane, depth, route_count, bool(run_d)),
            [row],
            move_flops,
            [place, step_ids[s]] + back_d[s] + run_d,
        )
        if not last:
            run_y = [hop(done_y[0], ring_up)]
            run_d = [hop(done_d[0], ring_up)]
    expert_out, gates = done_y
    grad_tokens = done_d[0]

    grads = call(
        functools.partial(grads_kernel, ring, plane),
        [shape(width, hidden_width), shape(width, hidden_width), shape(hidden_width, width)],
        3 * ring * dense_flops,
        [g for got in (got_x, got_c) for s in range(ring) for g in got[s]] + small,
    )
    return (
        expert_out,
        grad_tokens,
        gates[:route_count].T,
        grads[0][None],
        grads[1][None],
        grads[2][None],
    )


def solution(mesh):
    rows = P(("group", "owner"), None)
    stacked = P(("group", "owner"), None, None)
    weights = P("owner", None, None)

    return jax.shard_map(
        local,
        mesh=mesh,
        in_specs=(rows, rows, P("group", None), rows, weights, weights, weights),
        out_specs=(rows, rows, rows, stacked, stacked, stacked),
        check_vma=False,
    )
```

```python
import functools

import jax
import jax.numpy as jnp
from jax import lax
from jax.experimental import pallas as pl
from jax.experimental.pallas import tpu as pltpu
from jax.sharding import PartitionSpec as P


F32 = jnp.float32
BF16 = jnp.bfloat16
TILE = 512
VMEM = pl.BlockSpec(memory_space=pltpu.VMEM)
SMEM = pl.BlockSpec(memory_space=pltpu.SMEM)


def rounded(value):
    return value.astype(BF16).astype(F32)


def nt(a, b):
    return lax.dot_general(a, b, (((1,), (1,)), ((), ())), preferred_element_type=F32)


def nn(a, b):
    return jnp.dot(a, b, preferred_element_type=F32)


def expert_ids(place, plane):
    return [place[0] * plane + jnp.bitwise_xor(place[1], e) for e in range(plane)]


def block_ids(place, ids, tokens, step, plane, ring):
    origin = lax.rem(place[0] + (ring - step), ring)
    start = pl.multiple_of((origin * plane + place[1]) * tokens, tokens)
    return ids[:, pl.ds(start, tokens)]


def slots_of(place, ids, probs, plane, depth, route_count):
    tokens = ids.shape[1]
    rows = lax.broadcasted_iota(jnp.int32, (tokens, tokens), 0)
    cols = lax.broadcasted_iota(jnp.int32, (tokens, tokens), 1)
    before = jnp.where(rows < cols, 1.0, 0.0).astype(BF16)
    route = [ids[k : k + 1] for k in range(route_count)]
    slot = lax.broadcasted_iota(jnp.int32, (depth, tokens), 0)
    named, weight = [], []
    for eid in expert_ids(place, plane):
        hit = [jnp.where(r == eid, 1.0, 0.0) for r in route]
        named.append(sum(hit))
        if probs is not None:
            weight.append(sum(h * probs[k : k + 1] for k, h in enumerate(hit)))
    pad = [jnp.zeros((8 - plane % 8, tokens), F32)] if plane % 8 else []
    rank = nn(jnp.concatenate(named + pad, axis=0).astype(BF16), before)
    picks, gates = [], []
    for e in range(plane):
        wanted = jnp.broadcast_to(rank[e : e + 1], (depth, tokens)).astype(jnp.int32)
        present = jnp.broadcast_to(named[e], (depth, tokens))
        pick = jnp.where(wanted == slot, present, 0.0)
        picks.append(pick)
        if probs is not None:
            gates.append(jnp.sum(pick * weight[e], axis=1, keepdims=True))
    pick = jnp.concatenate(picks, axis=0)
    return pick, jnp.concatenate(gates, axis=0) if gates else None


def select_kernel(plane, ring, depth, step, scaled, place, ids, block, *outs):
    route_count = ids.shape[0]
    ids = block_ids(place, ids, block.shape[0], step, plane, ring)
    probs = None
    if scaled:
        probs, outs = outs[0][...], outs[1:]
    width = outs[0].shape[1]
    pick, gate = slots_of(place, ids, probs, plane, depth, route_count)
    chooser = pick.astype(BF16)
    for start in range(0, width, TILE):
        cols = pl.ds(start, TILE)
        found = nn(chooser, block[:, cols])
        if scaled:
            found = found * gate
        found = found.astype(BF16)
        for e in range(plane):
            outs[e][:, cols] = found[e * depth : (e + 1) * depth]


def forward_kernel(plane, *refs):
    rows = refs[:plane]
    gate_w, up_w, down_w = refs[plane : plane + 3]
    outs = refs[plane + 3 : 2 * plane + 3]
    hidden_out, gate_out, up_out = refs[2 * plane + 3 :]
    width = gate_w.shape[0]
    depth = rows[0].shape[0]
    row_x = jnp.concatenate([r[...] for r in rows], axis=0)
    gate_pre = nn(row_x, gate_w[...])
    up_pre = nn(row_x, up_w[...])
    gate_out[...] = gate_pre
    up_out[...] = up_pre
    gate_sig = 1.0 / (1.0 + jnp.exp(-gate_pre))
    hidden = (gate_pre * gate_sig * up_pre).astype(BF16)
    hidden_out[...] = hidden
    for start in range(0, width, TILE):
        cols = pl.ds(start, TILE)
        y = nn(hidden, down_w[:, cols]).astype(BF16)
        for e in range(plane):
            outs[e][:, cols] = y[e * depth : (e + 1) * depth]


def backward_kernel(plane, *refs):
    rows = refs[:plane]
    gate_pre, up_pre, gate_w, up_w, down_w = refs[plane : plane + 5]
    outs = refs[plane + 5 : 2 * plane + 5]
    ggp_out, gup_out = refs[2 * plane + 5 :]
    width = gate_w.shape[0]
    depth = rows[0].shape[0]
    row_c = jnp.concatenate([r[...] for r in rows], axis=0)
    d_hidden = nt(row_c, down_w[...])
    gate_pre = gate_pre[...]
    gate_sig = 1.0 / (1.0 + jnp.exp(-gate_pre))
    slope = gate_sig * (1.0 + gate_pre * (1.0 - gate_sig))
    ggp = (d_hidden * up_pre[...] * slope).astype(BF16)
    gup = (d_hidden * (gate_pre * gate_sig)).astype(BF16)
    ggp_out[...] = ggp
    gup_out[...] = gup
    for start in range(0, width, TILE):
        cols = pl.ds(start, TILE)
        dx = (nt(ggp, gate_w[cols, :]) + nt(gup, up_w[cols, :])).astype(BF16)
        for e in range(plane):
            outs[e][:, cols] = dx[e * depth : (e + 1) * depth]


def combine_out_kernel(plane, ring, depth, step, has_running, place, ids, block, *refs):
    tokens = block.shape[0]
    route_count = ids.shape[0]
    probs, refs = refs[0][...], refs[1:]
    near = refs[:plane]
    refs = refs[plane:]
    running = None
    if has_running:
        running, run_gates, refs = refs[0], refs[1], refs[2:]
    width = near[0].shape[1]
    ids_now = block_ids(place, ids, tokens, step, plane, ring)
    pick, gate = slots_of(place, ids_now, probs, plane, depth, route_count)
    weighted = pick * gate
    weight_high = rounded(weighted)
    high = jnp.transpose(weight_high).astype(BF16)
    low = jnp.transpose(weighted - weight_high).astype(BF16)
    dots = jnp.zeros((plane * depth, tokens), F32)
    for start in range(0, width, TILE):
        cols = pl.ds(start, TILE)
        y = jnp.concatenate([n[:, cols] for n in near], axis=0)
        part_y = nn(high, y) + nn(low, y)
        dots = dots + nt(y, block[:, cols])
        if has_running:
            part_y = part_y + running[:, cols].astype(F32)
        refs[0][:, cols] = part_y.astype(BF16)
    dots = pick * dots
    found = [jnp.sum(dots[e * depth : (e + 1) * depth], axis=0, keepdims=True) for e in range(plane)]
    gates = []
    for k in range(route_count):
        mine = ids_now[k : k + 1]
        total = jnp.zeros((1, tokens), F32)
        for eid, value in zip(expert_ids(place, plane), found):
            total = total + jnp.where(mine == eid, value, 0.0)
        gates.append(total)
    pad = jnp.zeros((8 - route_count, tokens), F32)
    total = jnp.concatenate(gates + [pad], axis=0)
    if has_running:
        total = total + run_gates[...]
    refs[1][...] = total


def combine_back_kernel(plane, ring, depth, step, has_running, place, ids, *refs):
    near = refs[:plane]
    out = refs[-1]
    route_count = ids.shape[0]
    ids = block_ids(place, ids, out.shape[0], step, plane, ring)
    width = near[0].shape[1]
    pick, _ = slots_of(place, ids, None, plane, depth, route_count)
    spread = jnp.transpose(pick).astype(BF16)
    for start in range(0, width, TILE):
        cols = pl.ds(start, TILE)
        dx = jnp.concatenate([n[:, cols] for n in near], axis=0)
        part_dx = nn(spread, dx)
        if has_running:
            part_dx = part_dx + refs[plane][:, cols].astype(F32)
        out[:, cols] = part_dx.astype(out.dtype)


def grads_kernel(ring, plane, *refs):
    count = ring * plane
    rows_x, rows_c = refs[:count], refs[count : 2 * count]
    small = refs[2 * count : 2 * count + 3 * ring]
    gate_out, up_out, down_out = refs[2 * count + 3 * ring :]
    width = gate_out.shape[0]
    hidden = jnp.transpose(jnp.concatenate([small[3 * s][...] for s in range(ring)], axis=0))
    ggp = jnp.concatenate([small[3 * s + 1][...] for s in range(ring)], axis=0)
    gup = jnp.concatenate([small[3 * s + 2][...] for s in range(ring)], axis=0)
    step = TILE // 2
    for start in range(0, width, step):
        cols = pl.ds(start, step)
        x = jnp.transpose(jnp.concatenate([r[:, cols] for r in rows_x], axis=0))
        gate_out[cols, :] = nn(x, ggp).astype(BF16)
        up_out[cols, :] = nn(x, gup).astype(BF16)
        c = jnp.concatenate([r[:, cols] for r in rows_c], axis=0)
        down_out[:, cols] = nn(hidden, c).astype(BF16)


def call(body, outs, flops, inputs):
    total = sum(x.size * x.dtype.itemsize for x in inputs)
    total += sum(o.size * o.dtype.itemsize for o in outs)
    specs = [SMEM if x.dtype == jnp.int32 and x.ndim == 1 else VMEM for x in inputs]
    return pl.pallas_call(
        body,
        out_shape=tuple(outs),
        in_specs=specs,
        out_specs=tuple(VMEM for _ in outs),
        cost_estimate=pl.CostEstimate(flops=flops, bytes_accessed=total, transcendentals=0),
        compiler_params=pltpu.CompilerParams(vmem_limit_bytes=40 * 1024 * 1024),
    )(*inputs)


def local(tokens, cotangent, route_ids, gate_probs, w_gate, w_up, w_down):
    owner_count = lax.axis_size("owner")
    me = lax.axis_index("owner")
    token_rows, width = tokens.shape
    route_count = route_ids.shape[1]
    hidden_width = w_gate.shape[2]
    depth = 2 * token_rows * route_count // owner_count
    depth = (depth + 15) // 16 * 16
    plane = 4 if owner_count % 4 == 0 else 2
    ring = owner_count // plane
    column = me % plane
    my_z = me // plane
    place = jnp.stack([my_z, column]).astype(jnp.int32)

    ring_up = [(i, (i + plane) % owner_count) for i in range(owner_count)]
    swaps = [[(i, i ^ e) for i in range(owner_count)] for e in range(plane)]

    def hop(value, pairs):
        return lax.ppermute(value, "owner", pairs)

    ids = route_ids.T
    block_x, block_c = [tokens], [cotangent]
    for _ in range(1, ring):
        block_x.append(hop(block_x[-1], ring_up))
        block_c.append(hop(block_c[-1], ring_up))
    probs = [jnp.pad(gate_probs.T, ((0, 8 - route_count), (0, 0)))]
    for _ in range(1, ring):
        probs.append(hop(probs[-1], ring_up))

    def shape(*dims, kind=BF16):
        return jax.ShapeDtypeStruct(dims, kind)

    rows = plane * depth
    slots = [shape(depth, width)] * plane
    weights = [w_gate[0], w_up[0], w_down[0]]
    move_flops = 2 * rows * token_rows * width
    dense_flops = 2 * rows * width * hidden_width

    def exchange(values):
        return [values[0]] + [hop(values[e], swaps[e]) for e in range(1, plane)]

    got_x, got_c, small = [], [], []
    back_y, back_d = [], []
    for s in range(ring):
        for blocks, got, extra in ((block_x, got_x, []), (block_c, got_c, [probs[s]])):
            picked = call(
                functools.partial(select_kernel, plane, ring, depth, s, bool(extra)),
                slots,
                move_flops,
                [place, ids, blocks[s]] + extra,
            )
            got.append(exchange(picked))
        ahead = call(
            functools.partial(forward_kernel, plane),
            slots + [shape(rows, hidden_width)] + [shape(rows, hidden_width, kind=F32)] * 2,
            3 * dense_flops,
            got_x[s] + weights,
        )
        back = call(
            functools.partial(backward_kernel, plane),
            slots + [shape(rows, hidden_width)] * 2,
            3 * dense_flops,
            got_c[s] + list(ahead[plane + 1 :]) + weights,
        )
        small += [ahead[plane], back[plane], back[plane + 1]]
        back_y.append(exchange(ahead[:plane]))
        back_d.append(exchange(back[:plane]))

    run_y, run_d, run_gates = [], [], []
    for s in list(range(1, ring)) + [0]:
        last = s == 0
        row = shape(token_rows, width)
        done_y = call(
            functools.partial(
                combine_out_kernel, plane, ring, depth, s, bool(run_y)
            ),
            [row, shape(8, token_rows, kind=F32)],
            3 * move_flops,
            [place, ids, block_c[s], probs[s]] + back_y[s] + run_y + run_gates,
        )
        before = [] if last else run_d
        done_d = call(
            functools.partial(combine_back_kernel, plane, ring, depth, s, bool(before)),
            [shape(token_rows, width, kind=F32) if last else row],
            move_flops,
            [place, ids] + back_d[s] + before,
        )
        if not last:
            run_y = [hop(done_y[0], ring_up)]
            run_d = [hop(done_d[0], ring_up)]
            run_gates = [hop(done_y[1], ring_up)]
    expert_out, gates = done_y
    grad_tokens = done_d[0]
    if run_d:
        grad_tokens = grad_tokens + run_d[0].astype(F32)
    grad_tokens = grad_tokens.astype(BF16)

    grads = call(
        functools.partial(grads_kernel, ring, plane),
        [shape(width, hidden_width), shape(width, hidden_width), shape(hidden_width, width)],
        3 * ring * dense_flops,
        [g for got in (got_x, got_c) for s in range(ring) for g in got[s]] + small,
    )
    return (
        expert_out,
        grad_tokens,
        gates[:route_count].T,
        grads[0][None],
        grads[1][None],
        grads[2][None],
    )


def solution(mesh):
    rows = P(("group", "owner"), None)
    stacked = P(("group", "owner"), None, None)
    weights = P("owner", None, None)

    return jax.shard_map(
        local,
        mesh=mesh,
        in_specs=(rows, rows, P("group", None), rows, weights, weights, weights),
        out_specs=(rows, rows, rows, stacked, stacked, stacked),
        check_vma=False,
    )
```

```python
import functools

import jax
import jax.numpy as jnp
from jax import lax
from jax.experimental import pallas as pl
from jax.experimental.pallas import tpu as pltpu
from jax.sharding import PartitionSpec as P


F32 = jnp.float32
BF16 = jnp.bfloat16
TILE = 512
VMEM = pl.BlockSpec(memory_space=pltpu.VMEM)
SMEM = pl.BlockSpec(memory_space=pltpu.SMEM)


def rounded(value):
    return value.astype(BF16).astype(F32)


def nt(a, b):
    return lax.dot_general(a, b, (((1,), (1,)), ((), ())), preferred_element_type=F32)


def nn(a, b):
    return jnp.dot(a, b, preferred_element_type=F32)


def expert_ids(place, plane):
    return [place[0] * plane + jnp.bitwise_xor(place[1], e) for e in range(plane)]


def block_ids(place, ids, tokens, step, plane, ring):
    origin = lax.rem(place[0] + (ring - step), ring)
    start = pl.multiple_of((origin * plane + place[1]) * tokens, tokens)
    return ids[:, pl.ds(start, tokens)]


def slots_of(place, ids, probs, plane, depth, route_count):
    tokens = ids.shape[1]
    rows = lax.broadcasted_iota(jnp.int32, (tokens, tokens), 0)
    cols = lax.broadcasted_iota(jnp.int32, (tokens, tokens), 1)
    before = jnp.where(rows < cols, 1.0, 0.0).astype(BF16)
    route = [ids[k : k + 1] for k in range(route_count)]
    slot = lax.broadcasted_iota(jnp.int32, (depth, tokens), 0)
    named, weight = [], []
    for eid in expert_ids(place, plane):
        hit = [jnp.where(r == eid, 1.0, 0.0) for r in route]
        named.append(sum(hit))
        if probs is not None:
            weight.append(sum(h * probs[k : k + 1] for k, h in enumerate(hit)))
    pad = [jnp.zeros((8 - plane % 8, tokens), F32)] if plane % 8 else []
    rank = nn(jnp.concatenate(named + pad, axis=0).astype(BF16), before)
    picks, gates = [], []
    for e in range(plane):
        wanted = jnp.broadcast_to(rank[e : e + 1], (depth, tokens)).astype(jnp.int32)
        present = jnp.broadcast_to(named[e], (depth, tokens))
        pick = jnp.where(wanted == slot, present, 0.0)
        picks.append(pick)
        if probs is not None:
            gates.append(jnp.sum(pick * weight[e], axis=1, keepdims=True))
    pick = jnp.concatenate(picks, axis=0)
    return pick, jnp.concatenate(gates, axis=0) if gates else None


def select_kernel(plane, ring, depth, step, scaled, place, ids, block, *outs):
    route_count = ids.shape[0]
    ids = block_ids(place, ids, block.shape[0], step, plane, ring)
    probs = None
    if scaled:
        probs, outs = outs[0][...], outs[1:]
    width = outs[0].shape[1]
    pick, gate = slots_of(place, ids, probs, plane, depth, route_count)
    chooser = pick.astype(BF16)
    for start in range(0, width, TILE):
        cols = pl.ds(start, TILE)
        found = nn(chooser, block[:, cols])
        if scaled:
            found = found * gate
        found = found.astype(BF16)
        for e in range(plane):
            outs[e][:, cols] = found[e * depth : (e + 1) * depth]


def forward_kernel(plane, *refs):
    rows = refs[:plane]
    gate_w, up_w, down_w = refs[plane : plane + 3]
    outs = refs[plane + 3 : -3]
    hidden_out, gate_out, up_out = refs[-3:]
    span = outs[0].shape[1]
    width = gate_w.shape[0]
    depth = rows[0].shape[0]
    row_x = jnp.concatenate([r[...] for r in rows], axis=0)
    gate_pre = nn(row_x, gate_w[...])
    up_pre = nn(row_x, up_w[...])
    gate_out[...] = gate_pre
    up_out[...] = up_pre
    gate_sig = 1.0 / (1.0 + jnp.exp(-gate_pre))
    hidden = (gate_pre * gate_sig * up_pre).astype(BF16)
    hidden_out[...] = hidden
    for start in range(0, width, TILE):
        cols = pl.ds(start, TILE)
        y = nn(hidden, down_w[:, cols]).astype(BF16)
        part = outs[start // span * plane :]
        for e in range(plane):
            part[e][:, pl.ds(start % span, TILE)] = y[e * depth : (e + 1) * depth]


def backward_kernel(plane, *refs):
    rows = refs[:plane]
    gate_pre, up_pre, gate_w, up_w, down_w = refs[plane : plane + 5]
    outs = refs[plane + 5 : 2 * plane + 5]
    ggp_out, gup_out = refs[2 * plane + 5 :]
    width = gate_w.shape[0]
    depth = rows[0].shape[0]
    row_c = jnp.concatenate([r[...] for r in rows], axis=0)
    d_hidden = nt(row_c, down_w[...])
    gate_pre = gate_pre[...]
    gate_sig = 1.0 / (1.0 + jnp.exp(-gate_pre))
    slope = gate_sig * (1.0 + gate_pre * (1.0 - gate_sig))
    ggp = (d_hidden * up_pre[...] * slope).astype(BF16)
    gup = (d_hidden * (gate_pre * gate_sig)).astype(BF16)
    ggp_out[...] = ggp
    gup_out[...] = gup
    for start in range(0, width, TILE):
        cols = pl.ds(start, TILE)
        dx = (nt(ggp, gate_w[cols, :]) + nt(gup, up_w[cols, :])).astype(BF16)
        for e in range(plane):
            outs[e][:, cols] = dx[e * depth : (e + 1) * depth]


def maps_kernel(plane, ring, depth, step, place, ids, probs, high, low, spread, picked):
    route_count = ids.shape[0]
    ids = block_ids(place, ids, probs.shape[1], step, plane, ring)
    pick, gate = slots_of(place, ids, probs[...], plane, depth, route_count)
    weighted = pick * gate
    weight_high = rounded(weighted)
    high[...] = jnp.transpose(weight_high).astype(BF16)
    low[...] = jnp.transpose(weighted - weight_high).astype(BF16)
    spread[...] = jnp.transpose(pick).astype(BF16)
    picked[...] = pick


def combine_kernel(plane, maps, runs, offset, *refs):
    weights = [r[...] for r in refs[:maps]]
    near = refs[maps : maps + plane]
    running = refs[maps + plane : maps + plane + runs]
    out = refs[-1]
    for start in range(0, near[0].shape[1], TILE):
        cols = pl.ds(start, TILE)
        rows = jnp.concatenate([n[:, cols] for n in near], axis=0)
        part = sum(nn(w, rows) for w in weights)
        if runs:
            span = running[0].shape[1]
            at = offset + start
            part = part + running[at // span][:, pl.ds(at % span, TILE)].astype(F32)
        out[:, cols] = part.astype(out.dtype)


def gates_kernel(plane, ring, depth, step, has_running, place, ids, picked, block, *refs):
    near = refs[: len(refs) - 1 - has_running]
    span = near[0].shape[1]
    out = refs[-1]
    tokens = block.shape[0]
    route_count = ids.shape[0]
    ids = block_ids(place, ids, tokens, step, plane, ring)
    dots = jnp.zeros((plane * depth, tokens), F32)
    for start in range(0, block.shape[1], TILE):
        cols = pl.ds(start % span, TILE)
        part = near[start // span * plane :][:plane]
        rows = jnp.concatenate([n[:, cols] for n in part], axis=0)
        dots = dots + nt(rows, block[:, pl.ds(start, TILE)])
    dots = picked[...] * dots
    found = [jnp.sum(dots[e * depth : (e + 1) * depth], axis=0, keepdims=True) for e in range(plane)]
    gates = []
    for k in range(route_count):
        total = jnp.zeros((1, tokens), F32)
        for eid, value in zip(expert_ids(place, plane), found):
            total = total + jnp.where(ids[k : k + 1] == eid, value, 0.0)
        gates.append(total)
    pad = jnp.zeros((8 - route_count, tokens), F32)
    total = jnp.concatenate(gates + [pad], axis=0)
    if has_running:
        total = total + refs[-2][...]
    out[...] = total


def grads_kernel(ring, plane, *refs):
    count = ring * plane
    rows_x, rows_c = refs[:count], refs[count : 2 * count]
    small = refs[2 * count : 2 * count + 3 * ring]
    gate_out, up_out, down_out = refs[2 * count + 3 * ring :]
    width = gate_out.shape[0]
    hidden = jnp.transpose(jnp.concatenate([small[3 * s][...] for s in range(ring)], axis=0))
    ggp = jnp.concatenate([small[3 * s + 1][...] for s in range(ring)], axis=0)
    gup = jnp.concatenate([small[3 * s + 2][...] for s in range(ring)], axis=0)
    step = TILE // 2
    for start in range(0, width, step):
        cols = pl.ds(start, step)
        x = jnp.transpose(jnp.concatenate([r[:, cols] for r in rows_x], axis=0))
        gate_out[cols, :] = nn(x, ggp).astype(BF16)
        up_out[cols, :] = nn(x, gup).astype(BF16)
        c = jnp.concatenate([r[:, cols] for r in rows_c], axis=0)
        down_out[:, cols] = nn(hidden, c).astype(BF16)


def call(body, outs, flops, inputs):
    total = sum(x.size * x.dtype.itemsize for x in inputs)
    total += sum(o.size * o.dtype.itemsize for o in outs)
    specs = [SMEM if x.dtype == jnp.int32 and x.ndim == 1 else VMEM for x in inputs]
    return pl.pallas_call(
        body,
        out_shape=tuple(outs),
        in_specs=specs,
        out_specs=tuple(VMEM for _ in outs),
        cost_estimate=pl.CostEstimate(flops=flops, bytes_accessed=total, transcendentals=0),
        compiler_params=pltpu.CompilerParams(vmem_limit_bytes=40 * 1024 * 1024),
    )(*inputs)


def local(tokens, cotangent, route_ids, gate_probs, w_gate, w_up, w_down):
    owner_count = lax.axis_size("owner")
    me = lax.axis_index("owner")
    token_rows, width = tokens.shape
    route_count = route_ids.shape[1]
    hidden_width = w_gate.shape[2]
    depth = 2 * token_rows * route_count // owner_count
    depth = (depth + 15) // 16 * 16
    plane = 4 if owner_count % 4 == 0 else 2
    ring = owner_count // plane
    column = me % plane
    my_z = me // plane
    place = jnp.stack([my_z, column]).astype(jnp.int32)

    ring_up = [(i, (i + plane) % owner_count) for i in range(owner_count)]
    swaps = [[(i, i ^ e) for i in range(owner_count)] for e in range(plane)]

    def hop(value, pairs):
        return lax.ppermute(value, "owner", pairs)

    ids = route_ids.T
    block_x, block_c = [tokens], [cotangent]
    for _ in range(1, ring):
        block_x.append(hop(block_x[-1], ring_up))
        block_c.append(hop(block_c[-1], ring_up))
    probs = [jnp.pad(gate_probs.T, ((0, 8 - route_count), (0, 0)))]
    for _ in range(1, ring):
        probs.append(hop(probs[-1], ring_up))

    def shape(*dims, kind=BF16):
        return jax.ShapeDtypeStruct(dims, kind)

    rows = plane * depth
    slots = [shape(depth, width)] * plane
    weights = [w_gate[0], w_up[0], w_down[0]]
    move_flops = 2 * rows * token_rows * width
    dense_flops = 2 * rows * width * hidden_width

    def exchange(values):
        return [values[0]] + [hop(values[e], swaps[e]) for e in range(1, plane)]

    got_x, got_c, small = [], [], []
    back_y, back_d = [], []
    for s in range(ring):
        for blocks, got, extra in ((block_x, got_x, []), (block_c, got_c, [probs[s]])):
            picked = call(
                functools.partial(select_kernel, plane, ring, depth, s, bool(extra)),
                slots,
                move_flops,
                [place, ids, blocks[s]] + extra,
            )
            got.append(exchange(picked))
        parts = 2 if ring > 1 and s == ring - 1 and width % (2 * TILE) == 0 else 1
        count = plane * parts
        ahead = call(
            functools.partial(forward_kernel, plane),
            [shape(depth, width // parts)] * count + [shape(rows, hidden_width)] + [shape(rows, hidden_width, kind=F32)] * 2,
            3 * dense_flops,
            got_x[s] + weights,
        )
        back = call(
            functools.partial(backward_kernel, plane),
            slots + [shape(rows, hidden_width)] * 2,
            3 * dense_flops,
            got_c[s] + list(ahead[count + 1 :]) + weights,
        )
        small += [ahead[count], back[plane], back[plane + 1]]
        back_y.append([exchange(ahead[p * plane : (p + 1) * plane]) for p in range(parts)])
        back_d.append(exchange(back[:plane]))

    run_y, run_d, run_gates = [], [], []
    for s in list(range(1, ring)) + [0]:
        last = s == 0
        high, low, spread, picked = call(
            functools.partial(maps_kernel, plane, ring, depth, s),
            [shape(token_rows, rows)] * 3 + [shape(rows, token_rows, kind=F32)],
            2 * 8 * token_rows * token_rows,
            [place, ids, probs[s]],
        )
        span = width // len(back_y[s])
        done_y = [
            call(
                functools.partial(combine_kernel, plane, 2, len(run_y), p * span),
                [shape(token_rows, span)],
                2 * move_flops * span // width,
                [high, low] + near + run_y,
            )[0]
            for p, near in enumerate(back_y[s])
        ]
        gates = call(
            functools.partial(gates_kernel, plane, ring, depth, s, bool(run_gates)),
            [shape(8, token_rows, kind=F32)],
            move_flops,
            [place, ids, picked, block_c[s]] + sum(back_y[s], []) + run_gates,
        )
        before = [] if last else run_d
        done_d = call(
            functools.partial(combine_kernel, plane, 1, len(before), 0),
            [shape(token_rows, width, kind=F32 if last else BF16)],
            move_flops,
            [spread] + back_d[s] + before,
        )
        if not last:
            run_y = [hop(y, ring_up) for y in done_y]
            run_d = [hop(done_d[0], ring_up)]
            run_gates = [hop(gates[0], ring_up)]
    expert_out, gates = done_y[0], gates[0]
    grad_tokens = done_d[0]
    if run_d:
        grad_tokens = grad_tokens + run_d[0].astype(F32)
    grad_tokens = grad_tokens.astype(BF16)

    grads = call(
        functools.partial(grads_kernel, ring, plane),
        [shape(width, hidden_width), shape(width, hidden_width), shape(hidden_width, width)],
        3 * ring * dense_flops,
        [g for got in (got_x, got_c) for s in range(ring) for g in got[s]] + small,
    )
    return (
        expert_out,
        grad_tokens,
        gates[:route_count].T,
        grads[0][None],
        grads[1][None],
        grads[2][None],
    )


def solution(mesh):
    rows = P(("group", "owner"), None)
    stacked = P(("group", "owner"), None, None)
    weights = P("owner", None, None)

    return jax.shard_map(
        local,
        mesh=mesh,
        in_specs=(rows, rows, P("group", None), rows, weights, weights, weights),
        out_specs=(rows, rows, rows, stacked, stacked, stacked),
        check_vma=False,
    )
```

```python
import functools

import jax
import jax.numpy as jnp
from jax import lax
from jax.experimental import pallas as pl
from jax.experimental.pallas import tpu as pltpu
from jax.sharding import PartitionSpec as P


F32 = jnp.float32
BF16 = jnp.bfloat16
TILE = 512
VMEM = pl.BlockSpec(memory_space=pltpu.VMEM)
SMEM = pl.BlockSpec(memory_space=pltpu.SMEM)


def rounded(value):
    return value.astype(BF16).astype(F32)


def nt(a, b):
    return lax.dot_general(a, b, (((1,), (1,)), ((), ())), preferred_element_type=F32)


def nn(a, b):
    return jnp.dot(a, b, preferred_element_type=F32)


def expert_ids(place, plane):
    return [place[0] * plane + jnp.bitwise_xor(place[1], e) for e in range(plane)]


def block_ids(place, ids, tokens, step, plane, ring):
    origin = lax.rem(place[0] + (ring - step), ring)
    start = pl.multiple_of((origin * plane + place[1]) * tokens, tokens)
    return ids[:, pl.ds(start, tokens)]


def slots_of(place, ids, probs, plane, depth, route_count):
    tokens = ids.shape[1]
    rows = lax.broadcasted_iota(jnp.int32, (tokens, tokens), 0)
    cols = lax.broadcasted_iota(jnp.int32, (tokens, tokens), 1)
    before = jnp.where(rows < cols, 1.0, 0.0).astype(BF16)
    route = [ids[k : k + 1] for k in range(route_count)]
    slot = lax.broadcasted_iota(jnp.int32, (depth, tokens), 0)
    named, weight = [], []
    for eid in expert_ids(place, plane):
        hit = [jnp.where(r == eid, 1.0, 0.0) for r in route]
        named.append(sum(hit))
        if probs is not None:
            weight.append(sum(h * probs[k : k + 1] for k, h in enumerate(hit)))
    pad = [jnp.zeros((8 - plane % 8, tokens), F32)] if plane % 8 else []
    rank = nn(jnp.concatenate(named + pad, axis=0).astype(BF16), before)
    picks, gates = [], []
    for e in range(plane):
        wanted = jnp.broadcast_to(rank[e : e + 1], (depth, tokens)).astype(jnp.int32)
        present = jnp.broadcast_to(named[e], (depth, tokens))
        pick = jnp.where(wanted == slot, present, 0.0)
        picks.append(pick)
        if probs is not None:
            gates.append(jnp.sum(pick * weight[e], axis=1, keepdims=True))
    pick = jnp.concatenate(picks, axis=0)
    return pick, jnp.concatenate(gates, axis=0) if gates else None


def select_kernel(plane, ring, depth, step, scaled, place, ids, block, *outs):
    route_count = ids.shape[0]
    ids = block_ids(place, ids, block.shape[0], step, plane, ring)
    probs = None
    if scaled:
        probs, outs = outs[0][...], outs[1:]
    width = outs[0].shape[1]
    pick, gate = slots_of(place, ids, probs, plane, depth, route_count)
    chooser = pick.astype(BF16)
    for start in range(0, width, TILE):
        cols = pl.ds(start, TILE)
        found = nn(chooser, block[:, cols])
        if scaled:
            found = found * gate
        found = found.astype(BF16)
        for e in range(plane):
            outs[e][:, cols] = found[e * depth : (e + 1) * depth]


def forward_kernel(plane, *refs):
    rows = refs[:plane]
    gate_w, up_w, down_w = refs[plane : plane + 3]
    outs = refs[plane + 3 : -3]
    hidden_out, gate_out, up_out = refs[-3:]
    span = outs[0].shape[1]
    width = gate_w.shape[0]
    depth = rows[0].shape[0]
    row_x = jnp.concatenate([r[...] for r in rows], axis=0)
    gate_pre = nn(row_x, gate_w[...])
    up_pre = nn(row_x, up_w[...])
    gate_out[...] = gate_pre
    up_out[...] = up_pre
    gate_sig = 1.0 / (1.0 + jnp.exp(-gate_pre))
    hidden = (gate_pre * gate_sig * up_pre).astype(BF16)
    hidden_out[...] = hidden
    for start in range(0, width, TILE):
        cols = pl.ds(start, TILE)
        y = nn(hidden, down_w[:, cols]).astype(BF16)
        part = outs[start // span * plane :]
        for e in range(plane):
            part[e][:, pl.ds(start % span, TILE)] = y[e * depth : (e + 1) * depth]


def backward_kernel(plane, *refs):
    rows = refs[:plane]
    gate_pre, up_pre, gate_w, up_w, down_w = refs[plane : plane + 5]
    outs = refs[plane + 5 : -2]
    ggp_out, gup_out = refs[-2:]
    span = outs[0].shape[1]
    width = gate_w.shape[0]
    depth = rows[0].shape[0]
    row_c = jnp.concatenate([r[...] for r in rows], axis=0)
    d_hidden = nt(row_c, down_w[...])
    gate_pre = gate_pre[...]
    gate_sig = 1.0 / (1.0 + jnp.exp(-gate_pre))
    slope = gate_sig * (1.0 + gate_pre * (1.0 - gate_sig))
    ggp = (d_hidden * up_pre[...] * slope).astype(BF16)
    gup = (d_hidden * (gate_pre * gate_sig)).astype(BF16)
    ggp_out[...] = ggp
    gup_out[...] = gup
    for start in range(0, width, TILE):
        cols = pl.ds(start, TILE)
        dx = (nt(ggp, gate_w[cols, :]) + nt(gup, up_w[cols, :])).astype(BF16)
        part = outs[start // span * plane :]
        for e in range(plane):
            part[e][:, pl.ds(start % span, TILE)] = dx[e * depth : (e + 1) * depth]


def maps_kernel(plane, ring, depth, step, place, ids, probs, high, low, spread, picked):
    route_count = ids.shape[0]
    ids = block_ids(place, ids, probs.shape[1], step, plane, ring)
    pick, gate = slots_of(place, ids, probs[...], plane, depth, route_count)
    weighted = pick * gate
    weight_high = rounded(weighted)
    high[...] = jnp.transpose(weight_high).astype(BF16)
    low[...] = jnp.transpose(weighted - weight_high).astype(BF16)
    spread[...] = jnp.transpose(pick).astype(BF16)
    picked[...] = pick


def combine_kernel(plane, maps, runs, offset, *refs):
    weights = [r[...] for r in refs[:maps]]
    near = refs[maps : maps + plane]
    running = refs[maps + plane : maps + plane + runs]
    out = refs[-1]
    for start in range(0, near[0].shape[1], TILE):
        cols = pl.ds(start, TILE)
        rows = jnp.concatenate([n[:, cols] for n in near], axis=0)
        part = sum(nn(w, rows) for w in weights)
        if runs:
            span = running[0].shape[1]
            at = offset + start
            part = part + running[at // span][:, pl.ds(at % span, TILE)].astype(F32)
        out[:, cols] = part.astype(out.dtype)


def gates_kernel(plane, ring, depth, step, has_running, place, ids, picked, block, *refs):
    near = refs[: len(refs) - 1 - has_running]
    span = near[0].shape[1]
    out = refs[-1]
    tokens = block.shape[0]
    route_count = ids.shape[0]
    ids = block_ids(place, ids, tokens, step, plane, ring)
    dots = jnp.zeros((plane * depth, tokens), F32)
    for start in range(0, block.shape[1], TILE):
        cols = pl.ds(start % span, TILE)
        part = near[start // span * plane :][:plane]
        rows = jnp.concatenate([n[:, cols] for n in part], axis=0)
        dots = dots + nt(rows, block[:, pl.ds(start, TILE)])
    dots = picked[...] * dots
    found = [jnp.sum(dots[e * depth : (e + 1) * depth], axis=0, keepdims=True) for e in range(plane)]
    gates = []
    for k in range(route_count):
        total = jnp.zeros((1, tokens), F32)
        for eid, value in zip(expert_ids(place, plane), found):
            total = total + jnp.where(ids[k : k + 1] == eid, value, 0.0)
        gates.append(total)
    pad = jnp.zeros((8 - route_count, tokens), F32)
    total = jnp.concatenate(gates + [pad], axis=0)
    if has_running:
        total = total + refs[-2][...]
    out[...] = total


def grads_kernel(ring, plane, *refs):
    count = ring * plane
    rows_x, rows_c = refs[:count], refs[count : 2 * count]
    small = refs[2 * count : 2 * count + 3 * ring]
    gate_out, up_out, down_out = refs[2 * count + 3 * ring :]
    width = gate_out.shape[0]
    hidden = jnp.transpose(jnp.concatenate([small[3 * s][...] for s in range(ring)], axis=0))
    ggp = jnp.concatenate([small[3 * s + 1][...] for s in range(ring)], axis=0)
    gup = jnp.concatenate([small[3 * s + 2][...] for s in range(ring)], axis=0)
    step = TILE // 2
    for start in range(0, width, step):
        cols = pl.ds(start, step)
        x = jnp.transpose(jnp.concatenate([r[:, cols] for r in rows_x], axis=0))
        gate_out[cols, :] = nn(x, ggp).astype(BF16)
        up_out[cols, :] = nn(x, gup).astype(BF16)
        c = jnp.concatenate([r[:, cols] for r in rows_c], axis=0)
        down_out[:, cols] = nn(hidden, c).astype(BF16)


def call(body, outs, flops, inputs):
    total = sum(x.size * x.dtype.itemsize for x in inputs)
    total += sum(o.size * o.dtype.itemsize for o in outs)
    specs = [SMEM if x.dtype == jnp.int32 and x.ndim == 1 else VMEM for x in inputs]
    return pl.pallas_call(
        body,
        out_shape=tuple(outs),
        in_specs=specs,
        out_specs=tuple(VMEM for _ in outs),
        cost_estimate=pl.CostEstimate(flops=flops, bytes_accessed=total, transcendentals=0),
        compiler_params=pltpu.CompilerParams(vmem_limit_bytes=40 * 1024 * 1024),
    )(*inputs)


def local(tokens, cotangent, route_ids, gate_probs, w_gate, w_up, w_down):
    owner_count = lax.axis_size("owner")
    me = lax.axis_index("owner")
    token_rows, width = tokens.shape
    route_count = route_ids.shape[1]
    hidden_width = w_gate.shape[2]
    depth = 2 * token_rows * route_count // owner_count
    depth = (depth + 15) // 16 * 16
    plane = 4 if owner_count % 4 == 0 else 2
    ring = owner_count // plane
    column = me % plane
    my_z = me // plane
    place = jnp.stack([my_z, column]).astype(jnp.int32)

    ring_up = [(i, (i + plane) % owner_count) for i in range(owner_count)]
    swaps = [[(i, i ^ e) for i in range(owner_count)] for e in range(plane)]

    def hop(value, pairs):
        return lax.ppermute(value, "owner", pairs)

    ids = route_ids.T
    block_x, block_c = [tokens], [cotangent]
    for _ in range(1, ring):
        block_x.append(hop(block_x[-1], ring_up))
        block_c.append(hop(block_c[-1], ring_up))
    probs = [jnp.pad(gate_probs.T, ((0, 8 - route_count), (0, 0)))]
    for _ in range(1, ring):
        probs.append(hop(probs[-1], ring_up))

    def shape(*dims, kind=BF16):
        return jax.ShapeDtypeStruct(dims, kind)

    rows = plane * depth
    slots = [shape(depth, width)] * plane
    weights = [w_gate[0], w_up[0], w_down[0]]
    move_flops = 2 * rows * token_rows * width
    dense_flops = 2 * rows * width * hidden_width

    def exchange(values):
        return [values[0]] + [hop(values[e], swaps[e]) for e in range(1, plane)]

    got_x, got_c, small = [], [], []
    back_y, back_d = [], []
    for s in range(ring):
        for blocks, got, extra in ((block_x, got_x, []), (block_c, got_c, [probs[s]])):
            picked = call(
                functools.partial(select_kernel, plane, ring, depth, s, bool(extra)),
                slots,
                move_flops,
                [place, ids, blocks[s]] + extra,
            )
            got.append(exchange(picked))
        parts = 2 if ring > 1 and s == ring - 1 and width % (2 * TILE) == 0 else 1
        count = plane * parts
        ahead = call(
            functools.partial(forward_kernel, plane),
            [shape(depth, width // parts)] * count + [shape(rows, hidden_width)] + [shape(rows, hidden_width, kind=F32)] * 2,
            3 * dense_flops,
            got_x[s] + weights,
        )
        back = call(
            functools.partial(backward_kernel, plane),
            [shape(depth, width // parts)] * count + [shape(rows, hidden_width)] * 2,
            3 * dense_flops,
            got_c[s] + list(ahead[count + 1 :]) + weights,
        )
        small += [ahead[count], back[count], back[count + 1]]
        back_y.append([exchange(ahead[p * plane : (p + 1) * plane]) for p in range(parts)])
        back_d.append([exchange(back[p * plane : (p + 1) * plane]) for p in range(parts)])

    run_y, run_d, run_gates = [], [], []
    for s in list(range(1, ring)) + [0]:
        last = s == 0
        high, low, spread, picked = call(
            functools.partial(maps_kernel, plane, ring, depth, s),
            [shape(token_rows, rows)] * 3 + [shape(rows, token_rows, kind=F32)],
            2 * 8 * token_rows * token_rows,
            [place, ids, probs[s]],
        )
        span = width // len(back_y[s])
        done_y = [
            call(
                functools.partial(combine_kernel, plane, 2, len(run_y), p * span),
                [shape(token_rows, span)],
                2 * move_flops * span // width,
                [high, low] + near + run_y,
            )[0]
            for p, near in enumerate(back_y[s])
        ]
        gates = call(
            functools.partial(gates_kernel, plane, ring, depth, s, bool(run_gates)),
            [shape(8, token_rows, kind=F32)],
            move_flops,
            [place, ids, picked, block_c[s]] + sum(back_y[s], []) + run_gates,
        )
        before = [] if last else run_d
        done_d = [
            call(
                functools.partial(combine_kernel, plane, 1, len(before), p * span),
                [shape(token_rows, span, kind=F32 if last else BF16)],
                move_flops * span // width,
                [spread] + near + before,
            )[0]
            for p, near in enumerate(back_d[s])
        ]
        if not last:
            run_y = [hop(y, ring_up) for y in done_y]
            run_d = [hop(d, ring_up) for d in done_d]
            run_gates = [hop(gates[0], ring_up)]
    expert_out, gates = done_y[0], gates[0]
    grad_tokens = done_d[0]
    if run_d:
        grad_tokens = grad_tokens + jnp.concatenate(run_d, axis=1).astype(F32)
    grad_tokens = grad_tokens.astype(BF16)

    grads = call(
        functools.partial(grads_kernel, ring, plane),
        [shape(width, hidden_width), shape(width, hidden_width), shape(hidden_width, width)],
        3 * ring * dense_flops,
        [g for got in (got_x, got_c) for s in range(ring) for g in got[s]] + small,
    )
    return (
        expert_out,
        grad_tokens,
        gates[:route_count].T,
        grads[0][None],
        grads[1][None],
        grads[2][None],
    )


def solution(mesh):
    rows = P(("group", "owner"), None)
    stacked = P(("group", "owner"), None, None)
    weights = P("owner", None, None)

    return jax.shard_map(
        local,
        mesh=mesh,
        in_specs=(rows, rows, P("group", None), rows, weights, weights, weights),
        out_specs=(rows, rows, rows, stacked, stacked, stacked),
        check_vma=False,
    )
```
